32 devices in a mesh: row: 8 (over z, y), col: 4 (over x, core).
Axes of the slice: x: 2, y: 2, z: 4, core: 2. Of those that a mesh axis runs over, the one named last changes fastest.
Arguments:
- image: bfloat16 [2048, 512], P(('row', 'col')), may hold values from -2 to 2
- text: bfloat16 [2048, 512], P(('row', 'col')), may hold values from -3 to 3
- logit_scale: float32 [1], replicated, may hold values from 10 to 100
Outputs:
- loss: float32 [1], replicated
- grad_image: float32 [2048, 512], P(('row', 'col'))
- grad_text: float32 [2048, 512], P(('row', 'col'))
The draws below stay inside these ranges and needn't reach their ends.
All inputs are finite; a program needn't handle non-finite values.
Results may differ from the reference program's by a relative error of at most 0.0095.
Values may be sent and summed in bfloat16 or wider, within the bound.
No kernel may reach another device: no remote copies, remote signals or barrier semaphores. Data moves between devices by JAX's collectives and lax.ppermute only.
A program may use at most 64 MiB of HBM per device.

```python
import jax
import jax.numpy as jnp
from jax import lax

E = 512
BATCH = 2048


def embed_pair(key):
    keys = jax.random.split(jax.random.fold_in(key, 11), 4)
    position = jnp.arange(BATCH)
    fraction = (position.astype(jnp.float32) / BATCH)[:, None]
    img_raw = jax.random.normal(keys[0], (BATCH, E), jnp.float32)
    agreement = 1.6 * (1.0 - fraction)
    noise = jax.random.normal(keys[1], (BATCH, E), jnp.float32)
    txt_raw = agreement * img_raw + noise
    img_scale = jnp.exp(jax.random.uniform(keys[2], (BATCH, 1), jnp.float32, -0.69, 0.69))
    txt_scale = jnp.exp(jax.random.uniform(keys[3], (BATCH, 1), jnp.float32, -0.69, 0.69))
    img_out = jnp.clip(img_raw * img_scale * 0.25, -2.0, 2.0)
    txt_out = jnp.clip(txt_raw * txt_scale * 0.25, -3.0, 3.0)
    return (img_out, txt_out)


def draw_image(key, part):
    return embed_pair(key)[0].astype(jnp.bfloat16)


def draw_text(key, part):
    return embed_pair(key)[1].astype(jnp.bfloat16)


def draw_logit_scale(key, part):
    return jax.random.uniform(jax.random.fold_in(key, 23), (1,), jnp.float32, 10.0, 30.0)


def setup_inputs(seed: int = 0) -> dict:
    key_list = jax.random.split(jax.random.key(seed), 4)
    return {
        "image": draw_image(jax.random.fold_in(key_list[3], 71), 0),
        "text": draw_text(jax.random.fold_in(key_list[3], 71), 0),
        "logit_scale": draw_logit_scale(jax.random.fold_in(key_list[3], 71), 0),
    }


def normalize(embedding):
    values = embedding.astype(jnp.float32)
    length = jnp.sqrt(lax.optimization_barrier(jnp.sum(values * values, axis=1, keepdims=True)) + 1e-06)
    return (values / length, length)

def unnormalize(unit_rows, length, gradient):
    return (gradient - unit_rows * lax.optimization_barrier(jnp.sum(unit_rows * gradient, axis=1, keepdims=True))) / length

def reference(image, text, logit_scale):
    sharpness = logit_scale[0]
    unit_image, image_len = normalize(image)
    unit_text, text_len = normalize(text)
    img_half = unit_image.astype(jnp.bfloat16)
    txt_half = unit_text.astype(jnp.bfloat16)
    block_rows = min(1024, BATCH)
    block_count = BATCH // block_rows
    img_blocks = img_half.reshape(block_count, block_rows, E)

    def stats(running, img_block):
        col_peak, col_sum = running
        logits = sharpness * jnp.dot(img_block, txt_half.T, preferred_element_type=jnp.float32)
        row_peak = lax.optimization_barrier(jnp.max(logits, axis=1))
        row_lse = row_peak + jnp.log(lax.optimization_barrier(jnp.sum(jnp.exp(logits - row_peak[:, None]), axis=1)))
        higher = jnp.maximum(col_peak, lax.optimization_barrier(jnp.max(logits, axis=0)))
        col_sum = col_sum * jnp.exp(col_peak - higher) + lax.optimization_barrier(jnp.sum(jnp.exp(logits - higher[None, :]), axis=0))
        return ((higher, col_sum), row_lse)
    lowest = jnp.full((BATCH,), -1e+30, jnp.float32)
    (col_peak, col_sum), row_lse = lax.scan(stats, (lowest, jnp.zeros((BATCH,), jnp.float32)), img_blocks)
    row_lse = row_lse.reshape(BATCH)
    col_lse = col_peak + jnp.log(col_sum)
    positive = sharpness * lax.optimization_barrier(jnp.sum(img_half.astype(jnp.float32) * txt_half.astype(jnp.float32), axis=1))
    loss = ((jnp.sum(row_lse - positive) + jnp.sum(col_lse - positive)) / (2 * BATCH)).reshape(1)

    def backward(running, inputs):
        img_block, lse_rows = inputs
        logits = sharpness * jnp.dot(img_block, txt_half.T, preferred_element_type=jnp.float32)
        weights = (0.5 * (jnp.exp(logits - lse_rows[:, None]) + jnp.exp(logits - col_lse[None, :]))).astype(jnp.bfloat16)
        img_grad = sharpness * jnp.dot(weights, txt_half, preferred_element_type=jnp.float32)
        running = running + sharpness * jnp.dot(weights.T, img_block, preferred_element_type=jnp.float32)
        return (running, img_grad)
    txt_grad, img_grad = lax.scan(backward, jnp.zeros((BATCH, E), jnp.float32), (img_blocks, row_lse.reshape(block_count, block_rows)))
    img_grad = img_grad.reshape(BATCH, E) - sharpness * txt_half.astype(jnp.float32)
    txt_grad = txt_grad - sharpness * img_half.astype(jnp.float32)
    return (loss, unnormalize(unit_image, image_len, img_grad), unnormalize(unit_text, text_len, txt_grad))
```

```python
import jax
import jax.numpy as jnp
from jax import lax
from jax.sharding import PartitionSpec as P

AXES = ("row", "col")


def split(chips):
    bits = chips.bit_length() - 1
    images = 1 << (bits // 2)
    return images, chips // images


def permutes(devices):
    images, texts = split(devices // 2)
    core = [(i, i ^ 1) for i in range(devices)]
    groups = []
    for k in range(1, max(images, texts)):
        pairs = []
        for i in range(devices):
            if i & 1 == 0 and k < images:
                pairs.append((i, i ^ (k << 1)))
            if i & 1 == 1 and k < texts:
                pairs.append((i, i ^ (k * images << 1)))
        groups.append(pairs)
    return core, groups


def normalize(embedding):
    values = embedding.astype(jnp.float32)
    length = jnp.sqrt(jnp.sum(values * values, axis=1, keepdims=True) + 1e-06)
    return (values / length, length)


def unnormalize(unit_rows, length, gradient):
    return (gradient - unit_rows * jnp.sum(unit_rows * gradient, axis=1, keepdims=True)) / length


def on_device(image, text, logit_scale):
    devices = lax.axis_size("row") * lax.axis_size("col")
    images, texts = split(devices // 2)
    blocks = max(images, texts)
    even = images == texts
    core_pairs, group_pairs = permutes(devices)
    core_swap = lambda value: lax.ppermute(value, AXES, core_pairs)
    on_group = lambda value, k: lax.ppermute(value, AXES, group_pairs[k - 1])

    own = image.shape[0]
    pair = 2 * own
    sharpness = logit_scale[0]
    first = lax.axis_index("col") % 2 == 0
    raw_a = jnp.where(first, image, text)
    raw_b = jnp.where(first, text, image)
    unit_a, len_a = normalize(raw_a)
    unit_b, len_b = normalize(raw_b)
    mine = jnp.concatenate([unit_a, unit_b]).astype(jnp.bfloat16)
    other = core_swap(mine)
    a_blocks = [jnp.concatenate([mine[:own], other[own:]])]
    b_blocks = [jnp.concatenate([other[:own], mine[own:]])]
    for k in range(1, blocks):
        a_blocks.append(on_group(a_blocks[0], k))
    for k in range(1, blocks):
        b_blocks.append(core_swap(a_blocks[k]))
    count_a = jnp.where(first, images, texts)
    count_b = jnp.where(first, texts, images)
    a_side = jnp.concatenate(a_blocks)
    b_side = jnp.concatenate(b_blocks)
    logits = sharpness * jnp.einsum("ae,be->ab", a_side, b_side, preferred_element_type=jnp.float32)
    if not even:
        known = jnp.arange(blocks * pair) < count_b * pair
        logits = jnp.where(known[None, :], logits, -1e30)
    peak = jnp.max(logits, axis=1)
    total = jnp.sum(jnp.exp(logits - peak[:, None]), axis=1)
    positive = sharpness * jnp.sum(
        a_blocks[0].astype(jnp.float32) * jnp.roll(b_blocks[0], own, axis=0).astype(jnp.float32), axis=1
    )
    stats = jnp.concatenate([peak.reshape(blocks, pair), total.reshape(blocks, pair), positive[None]])
    peaks, totals, positives = [stats[:blocks]], [stats[blocks : 2 * blocks]], [positive]
    for k in range(1, blocks):
        got = on_group(stats, k)
        order = jnp.array([j ^ k for j in range(blocks)])
        peaks.append(jnp.where(k < count_a, got[:blocks][order], -1e30))
        totals.append(got[blocks : 2 * blocks][order])
        positives.append(got[2 * blocks])
    highest = peaks[0]
    for p in peaks[1:]:
        highest = jnp.maximum(highest, p)
    lse_a = highest + jnp.log(sum(t * jnp.exp(p - highest) for p, t in zip(peaks, totals)))
    excess = jnp.where((jnp.arange(blocks) < count_a)[:, None], lse_a - jnp.stack(positives), 0.0)
    swapped = core_swap(jnp.concatenate([lse_a, jnp.broadcast_to(jnp.sum(excess), (1, pair))]))
    lse_b = swapped[:blocks].reshape(-1)
    part = swapped[blocks, 0]
    lse_a = lse_a.reshape(-1)
    spot = jnp.arange(blocks * pair)
    at = jnp.where(spot < pair, (spot + own) % pair, -1)
    weights = 0.5 * (jnp.exp(logits - lse_a[:, None]) + jnp.exp(logits - lse_b[None, :]))
    if not even:
        weights = jnp.where(known[None, :], weights, 0.0)
    weights = (weights - (at[:, None] == spot[None, :]).astype(jnp.float32)).astype(jnp.bfloat16)
    partial = sharpness * jnp.dot(weights, b_side, preferred_element_type=jnp.float32)
    partial = partial.reshape(blocks, pair, -1)
    pieces = []
    rest = part
    for _ in range(3):
        piece = lax.reduce_precision(rest, 8, 7)
        pieces.append(piece)
        rest = rest - piece
    tail = jnp.broadcast_to(jnp.stack(pieces + [rest * 0.0] * 5)[:, None], (8, partial.shape[2]))
    gradient = partial[0]
    for k in range(1, blocks):
        got = on_group(jnp.concatenate([partial[k], tail]).astype(jnp.bfloat16), k).astype(jnp.float32)
        gradient = gradient + got[:pair]
        part = part + (got[pair, 0] + got[pair + 1, 0] + got[pair + 2, 0])
    tail = jnp.broadcast_to(part, (8, partial.shape[2]))
    final = core_swap(jnp.concatenate([gradient[own:], tail]))
    loss = ((part + final[own, 0]) / (2 * own * devices)).reshape(1)
    grad_a = unnormalize(unit_a, len_a, gradient[:own])
    grad_b = unnormalize(unit_b, len_b, final[:own])
    return (loss, jnp.where(first, grad_a, grad_b), jnp.where(first, grad_b, grad_a))


def solution(mesh):
    placed = (P(AXES, None), P(AXES, None), P())
    return jax.shard_map(
        on_device,
        mesh=mesh,
        in_specs=placed,
        out_specs=(P(), P(AXES, None), P(AXES, None)),
        check_vma=False,
    )
```

```python
import functools

import jax
import jax.numpy as jnp
from jax import lax
from jax.experimental import pallas as pl
from jax.experimental.pallas import tpu as pltpu
from jax.sharding import PartitionSpec as P

AXES = ("row", "col")
F32, BF16 = jnp.float32, jnp.bfloat16
VMEM = pl.BlockSpec(memory_space=pltpu.VMEM)
SMEM = pl.BlockSpec(memory_space=pltpu.SMEM)
TAIL = 16


def split(chips):
    bits = chips.bit_length() - 1
    images = 1 << (bits // 2)
    return images, chips // images


def permutes(devices):
    images, texts = split(devices // 2)
    core = [(i, i ^ 1) for i in range(devices)]
    groups = []
    for k in range(1, max(images, texts)):
        pairs = []
        for i in range(devices):
            if i & 1 == 0 and k < images:
                pairs.append((i, i ^ (k << 1)))
            if i & 1 == 1 and k < texts:
                pairs.append((i, i ^ (k * images << 1)))
        groups.append(pairs)
    return core, groups


def normalize(embedding):
    values = embedding.astype(F32)
    length = jnp.sqrt(jnp.sum(values * values, axis=1, keepdims=True) + 1e-06)
    return (values / length, length)


def unnormalize(unit_rows, length, gradient):
    return (gradient - unit_rows * jnp.sum(unit_rows * gradient, axis=1, keepdims=True)) / length


def is_first():
    return lax.axis_index("col") % 2 == 0


def counts(images, texts):
    first = is_first()
    return jnp.where(first, images, texts), jnp.where(first, texts, images)


def call(kernel, outs, args, specs=None, out_specs=None, cost=None):
    return pl.pallas_call(
        kernel,
        out_shape=outs,
        in_specs=specs or [VMEM] * len(args),
        out_specs=out_specs or jax.tree.map(lambda _: VMEM, outs),
        cost_estimate=cost,
        compiler_params=pltpu.CompilerParams(vmem_limit_bytes=48 << 20),
    )(*args)


def shape(dims, dtype=F32):
    return jax.ShapeDtypeStruct(dims, dtype)


def prepare_kernel(image, text, other_image, other_text, scale, a_chip, b_chip, scale_row):
    own = image.shape[0]
    first = is_first()
    img, txt = normalize(image[...])[0].astype(BF16), normalize(text[...])[0].astype(BF16)
    img_far, txt_far = normalize(other_image[...])[0].astype(BF16), normalize(other_text[...])[0].astype(BF16)
    scale_row[...] = jnp.full(scale_row.shape, scale[0], F32)

    @pl.when(first)
    def _():
        a_chip[0:own], a_chip[own:] = img, img_far
        b_chip[0:own], b_chip[own:] = txt_far, txt

    @pl.when(jnp.logical_not(first))
    def _():
        a_chip[0:own], a_chip[own:] = txt, txt_far
        b_chip[0:own], b_chip[own:] = img_far, img


def stats_kernel(images, texts, *refs):
    n = max(images, texts)
    a_in, b_in, scale, stats, a_all, b_all = refs[:n], refs[n : 2 * n], *refs[2 * n :]
    pair = a_in[0].shape[0]
    for k in range(n):
        a_all[k * pair : (k + 1) * pair] = a_in[k][...]
        b_all[k * pair : (k + 1) * pair] = b_in[k][...]
    s = scale[0:1]
    count_b = counts(images, texts)[1]
    for k in range(n):
        here = slice(k * pair, (k + 1) * pair)
        logits = s * lax.dot_general(
            b_all[...], a_in[k][...], (((1,), (1,)), ((), ())), preferred_element_type=F32
        )
        if images != texts:
            rows = lax.broadcasted_iota(jnp.int32, logits.shape, 0)
            logits = jnp.where(rows < count_b * pair, logits, -1e30)
        peak = jnp.max(logits, axis=0, keepdims=True)
        stats[0:1, here] = peak
        stats[1:2, here] = jnp.sum(jnp.exp(logits - peak), axis=0, keepdims=True)
        if k == 0:
            row = lax.broadcasted_iota(jnp.int32, (pair, pair), 0)
            col = lax.broadcasted_iota(jnp.int32, (pair, pair), 1)
            paired = row == lax.rem(col + pair // 2, pair)
            stats[2:3, here] = jnp.sum(jnp.where(paired, logits[:pair], 0.0), axis=0, keepdims=True)


def logits_kernel(a_all, b_all, scale, logits):
    rows = scale.shape[1]
    for k in range(a_all.shape[0] // rows):
        here = slice(k * rows, (k + 1) * rows)
        logits[here] = scale[0:1, 0:1] * lax.dot_general(
            a_all[here], b_all[...], (((1,), (1,)), ((), ())), preferred_element_type=F32
        )


def combine_kernel(images, texts, *refs):
    n = max(images, texts)
    got, message, column = refs[:n], *refs[n:]
    pair = message.shape[1] // n
    count_a = counts(images, texts)[0]
    excess = jnp.zeros((1, pair), F32)
    for j in range(n):
        here = slice(j * pair, (j + 1) * pair)
        peaks, totals = [], []
        for k in range(n):
            there = slice((j ^ k) * pair, ((j ^ k) + 1) * pair)
            peak = got[k][0:1, there]
            peaks.append(jnp.where(k < count_a, peak, -1e30) if images != texts else peak)
            totals.append(got[k][1:2, there])
        highest = functools.reduce(jnp.maximum, peaks)
        lse = highest + jnp.log(sum(t * jnp.exp(p - highest) for p, t in zip(peaks, totals)))
        message[0:1, here] = lse
        column[here] = jnp.broadcast_to(lse, (pair, pair)).T
        over = lse - got[j][2:3, 0:pair]
        excess = excess + (jnp.where(j < count_a, over, 0.0) if images != texts else over)
    message[1:2] = jnp.broadcast_to(jnp.sum(excess, axis=1, keepdims=True), (1, message.shape[1]))


def weigh(images, texts, k, logits, column, lse_b, b_all, scale):
    n = max(images, texts)
    pair = column.shape[1]
    here = slice(k * pair, (k + 1) * pair)
    count_b = counts(images, texts)[1]
    parts = []
    for j in range(n):
        there = slice(j * pair, (j + 1) * pair)
        block = logits[here, there]
        part = 0.5 * (jnp.exp(block - column[here]) + jnp.exp(block - lse_b[0:1, there]))
        if images != texts:
            part = jnp.where(j < count_b, part, 0.0)
        if k == 0 and j == 0:
            row = lax.broadcasted_iota(jnp.int32, (pair, pair), 0)
            col = lax.broadcasted_iota(jnp.int32, (pair, pair), 1)
            part = part - (col == lax.rem(row + pair // 2, pair)).astype(F32)
        parts.append(part.astype(BF16))
    weights = jnp.concatenate(parts, axis=1)
    return scale[0:1, 0:1] * jnp.dot(weights, b_all[...], preferred_element_type=F32)


def send_kernel(images, texts, logits, column, lse_b, b_all, scale, *outs):
    pair, width = column.shape[1], b_all.shape[1]
    rest = jnp.max(lse_b[1:2], axis=1, keepdims=True)
    row = lax.broadcasted_iota(jnp.int32, (TAIL, width), 0)
    tail = jnp.zeros((TAIL, width), F32)
    for i in range(3):
        piece = rest.astype(BF16).astype(F32)
        tail = jnp.where(row == i, piece, tail)
        rest = rest - piece
    tail = tail.astype(BF16)
    for k, out in enumerate(outs, 1):
        out[0:pair] = weigh(images, texts, k, logits, column, lse_b, b_all, scale).astype(BF16)
        out[pair:] = tail


def keep_kernel(images, texts, logits, column, lse_b, b_all, scale, out):
    out[...] = weigh(images, texts, 0, logits, column, lse_b, b_all, scale)


def reduce_kernel(images, texts, image, text, kept, lse_b, *refs):
    n = max(images, texts)
    got, message, grad_a = refs[: n - 1], *refs[n - 1 :]
    pair = kept.shape[0]
    own = pair // 2
    first = is_first()
    total = kept[...]
    excess = lse_b[1:2, 0:1]
    for ref in got:
        total = total + ref[0:pair].astype(F32)
        excess = excess + jnp.sum(ref[pair:].astype(F32), axis=0, keepdims=True)[:, 0:1]
    message[0:own] = total[own:]
    message[own:] = jnp.broadcast_to(excess, (8, message.shape[1]))
    unit, length = normalize(jnp.where(first, image[...].astype(F32), text[...].astype(F32)))
    grad_a[...] = unnormalize(unit, length, total[:own])


def finish_kernel(batch, image, text, message, grad_a, received, loss, grad_image, grad_text):
    own = image.shape[0]
    first = is_first()
    total = jnp.sum(message[own : own + 1, 0:1]) + jnp.sum(received[own : own + 1, 0:1])
    loss[0] = total / (2 * batch)
    unit, length = normalize(jnp.where(first, text[...].astype(F32), image[...].astype(F32)))
    grad_b = unnormalize(unit, length, received[:own])

    @pl.when(first)
    def _():
        grad_image[...] = grad_a[...]
        grad_text[...] = grad_b

    @pl.when(jnp.logical_not(first))
    def _():
        grad_image[...] = grad_b
        grad_text[...] = grad_a[...]


def on_device(image, text, logit_scale):
    devices = lax.axis_size("row") * lax.axis_size("col")
    images, texts = split(devices // 2)
    n = max(images, texts)
    core_pairs, group_pairs = permutes(devices)
    swap = lambda value: lax.ppermute(value, AXES, core_pairs)
    on_group = lambda value, k: lax.ppermute(value, AXES, group_pairs[k - 1])
    own, width = image.shape
    pair = 2 * own
    side = n * pair

    a_chip, b_chip, scale = call(
        prepare_kernel,
        (shape((pair, width), BF16), shape((pair, width), BF16), shape((8, pair))),
        (image, text, swap(image), swap(text), logit_scale),
        [VMEM] * 4 + [SMEM],
    )
    a_blocks = [a_chip] + [on_group(a_chip, k) for k in range(1, n)]
    b_blocks = [b_chip] + [swap(a) for a in a_blocks[1:]]
    stats, a_all, b_all = call(
        functools.partial(stats_kernel, images, texts),
        (shape((8, side)), shape((side, width), BF16), shape((side, width), BF16)),
        (*a_blocks, *b_blocks, scale),
    )
    got = [stats] + [on_group(stats, k) for k in range(1, n)]
    matmul = pl.CostEstimate(
        flops=2 * side * side * width, transcendentals=0, bytes_accessed=4 * side * side
    )
    logits = call(logits_kernel, shape((side, side)), (a_all, b_all, scale), cost=matmul)
    lse_message, column = call(
        functools.partial(combine_kernel, images, texts),
        (shape((8, side)), shape((side, pair))),
        tuple(got),
    )
    lse_b = swap(lse_message)
    inputs = (logits, column, lse_b, b_all, scale)
    sends = call(
        functools.partial(send_kernel, images, texts),
        tuple(shape((pair + TAIL, width), BF16) for _ in range(1, n)),
        inputs,
    )
    received = [on_group(sends[k - 1], k) for k in range(1, n)]
    kept = call(
        functools.partial(keep_kernel, images, texts), shape((pair, width)), inputs, cost=matmul
    )
    message, grad_a = call(
        functools.partial(reduce_kernel, images, texts),
        (shape((own + 8, width)), shape((own, width))),
        (image, text, kept, lse_b, *received),
    )
    return call(
        functools.partial(finish_kernel, own * devices),
        (shape((1,)), shape((own, width)), shape((own, width))),
        (image, text, message, grad_a, swap(message)),
        out_specs=(SMEM, VMEM, VMEM),
    )


def solution(mesh):
    placed = (P(AXES, None), P(AXES, None), P())
    return jax.shard_map(
        on_device,
        mesh=mesh,
        in_specs=placed,
        out_specs=(P(), P(AXES, None), P(AXES, None)),
        check_vma=False,
    )
```

```python
import functools

import jax
import jax.numpy as jnp
from jax import lax
from jax.experimental import pallas as pl
from jax.experimental.pallas import tpu as pltpu
from jax.sharding import PartitionSpec as P

AXES = ("row", "col")
F32, BF16 = jnp.float32, jnp.bfloat16
VMEM = pl.BlockSpec(memory_space=pltpu.VMEM)
SMEM = pl.BlockSpec(memory_space=pltpu.SMEM)
TAIL = 16


def split(chips):
    bits = chips.bit_length() - 1
    images = 1 << (bits // 2)
    return images, chips // images


IMAGE_BASIS = (3, 1)
TEXT_BASIS = (3, 1)


def member(k, basis):
    mask = 0
    for bit in range(k.bit_length()):
        if k >> bit & 1:
            mask ^= basis[bit] if bit < len(basis) else 1 << bit
    return mask


def permutes(devices):
    images, texts = split(devices // 2)
    image_basis = IMAGE_BASIS if images >= 4 else ()
    text_basis = TEXT_BASIS if texts >= 4 else ()
    core = [(i, i ^ 1) for i in range(devices)]
    groups = []
    for k in range(1, max(images, texts)):
        pairs = []
        for i in range(devices):
            if i & 1 == 0 and k < images:
                pairs.append((i, i ^ (member(k, image_basis) << 1)))
            if i & 1 == 1 and k < texts:
                pairs.append((i, i ^ (member(k, text_basis) * images << 1)))
        groups.append(pairs)
    return core, groups


def normalize(embedding):
    values = embedding.astype(F32)
    length = jnp.sqrt(jnp.sum(values * values, axis=1, keepdims=True) + 1e-06)
    return (values / length, length)


def unnormalize(unit_rows, length, gradient):
    return (gradient - unit_rows * jnp.sum(unit_rows * gradient, axis=1, keepdims=True)) / length


def is_first():
    return lax.axis_index("col") % 2 == 0


def counts(images, texts):
    first = is_first()
    return jnp.where(first, images, texts), jnp.where(first, texts, images)


def call(kernel, outs, args, specs=None, out_specs=None, cost=None, scratch=(), limit=48 << 20):
    return pl.pallas_call(
        kernel,
        out_shape=outs,
        in_specs=specs or [VMEM] * len(args),
        out_specs=out_specs or jax.tree.map(lambda _: VMEM, outs),
        scratch_shapes=scratch,
        cost_estimate=cost,
        compiler_params=pltpu.CompilerParams(vmem_limit_bytes=limit),
    )(*args)


def shape(dims, dtype=F32):
    return jax.ShapeDtypeStruct(dims, dtype)


def load_kernel(image_hbm, text_hbm, image, text, own_image, own_text, arrived):
    copies = [
        pltpu.make_async_copy(source, target, arrived.at[i])
        for i, (source, target) in enumerate(((image_hbm, image), (text_hbm, text)))
    ]
    for copy in copies:
        copy.start()
    copies[0].wait()
    own_image[...] = normalize(image[...])[0].astype(BF16)
    copies[1].wait()
    own_text[...] = normalize(text[...])[0].astype(BF16)


def prepare_kernel(image, text, other_image, other_text, a_chip, b_chip):
    own = image.shape[0]
    img, txt = image[...], text[...]
    img_far, txt_far = normalize(other_image[...])[0].astype(BF16), normalize(other_text[...])[0].astype(BF16)
    first = is_first()

    @pl.when(first)
    def _():
        a_chip[0:own], a_chip[own:] = img, img_far
        b_chip[0:own], b_chip[own:] = txt_far, txt

    @pl.when(jnp.logical_not(first))
    def _():
        a_chip[0:own], a_chip[own:] = txt, txt_far
        b_chip[0:own], b_chip[own:] = img_far, img


def stats_kernel(images, texts, n_b, *refs):
    n = max(images, texts)
    last = n_b == 1 and n > 1
    a_in, b_in, rest = refs[:n], refs[n : n + n_b], refs[n + n_b :]
    before = rest[0] if last else None
    scale, stats = rest[-2:]
    pair = a_in[0].shape[0]
    s = scale[0]
    count_b = counts(images, texts)[1]
    for k in range(n):
        here = slice(k * pair, (k + 1) * pair)
        blocks = []
        for j in range(n_b):
            block = s * lax.dot_general(
                b_in[j][...], a_in[k][...], (((1,), (1,)), ((), ())), preferred_element_type=F32
            )
            if images != texts:
                block = jnp.where((n - 1 if last else j) < count_b, block, -1e30)
            blocks.append(block)
        peak = functools.reduce(jnp.maximum, blocks)
        peak = jnp.max(peak, axis=0, keepdims=True)
        if last:
            peak = jnp.maximum(peak, before[0:1, here])
        total = sum(jnp.exp(block - peak) for block in blocks)
        total = jnp.sum(total, axis=0, keepdims=True)
        if last:
            total = total + before[1:2, here] * jnp.exp(before[0:1, here] - peak)
        stats[0:1, here] = peak
        stats[1:2, here] = total
        if k == 0 and last:
            stats[2:3, here] = before[2:3, here]
        elif k == 0:
            row = lax.broadcasted_iota(jnp.int32, (pair, pair), 0)
            col = lax.broadcasted_iota(jnp.int32, (pair, pair), 1)
            paired = row == lax.rem(col + pair // 2, pair)
            stats[2:3, here] = jnp.sum(jnp.where(paired, blocks[0], 0.0), axis=0, keepdims=True)


def logits_kernel(n, *refs):
    a_in, b_in, (scale, logits, b_all) = refs[:n], refs[n : 2 * n], refs[2 * n :]
    pair = a_in[0].shape[0]
    for k in range(n):
        b_all[k * pair : (k + 1) * pair] = b_in[k][...]
    for k in range(n):
        logits[k * pair : (k + 1) * pair] = scale[0] * lax.dot_general(
            a_in[k][...], b_all[...], (((1,), (1,)), ((), ())), preferred_element_type=F32
        )


def combine_kernel(images, texts, *refs):
    n = max(images, texts)
    got, message, column = refs[:n], *refs[n:]
    pair = message.shape[1] // n
    count_a = counts(images, texts)[0]
    excess = jnp.zeros((1, pair), F32)
    for j in range(n):
        here = slice(j * pair, (j + 1) * pair)
        peaks, totals = [], []
        for k in range(n):
            there = slice((j ^ k) * pair, ((j ^ k) + 1) * pair)
            peak = got[k][0:1, there]
            peaks.append(jnp.where(k < count_a, peak, -1e30) if images != texts else peak)
            totals.append(got[k][1:2, there])
        highest = functools.reduce(jnp.maximum, peaks)
        lse = highest + jnp.log(sum(t * jnp.exp(p - highest) for p, t in zip(peaks, totals)))
        message[0:1, here] = lse
        column[here] = jnp.broadcast_to(lse, (pair, pair)).T
        over = lse - got[j][2:3, 0:pair]
        excess = excess + (jnp.where(j < count_a, over, 0.0) if images != texts else over)
    message[1:2] = jnp.broadcast_to(jnp.sum(excess, axis=1, keepdims=True), (1, message.shape[1]))


def weigh(images, texts, k, logits, column, lse_b, b_all, scale):
    n = max(images, texts)
    pair = column.shape[1]
    here = slice(k * pair, (k + 1) * pair)
    count_b = counts(images, texts)[1]
    parts = []
    for j in range(n):
        there = slice(j * pair, (j + 1) * pair)
        block = logits[here, there]
        part = 0.5 * (jnp.exp(block - column[here]) + jnp.exp(block - lse_b[0:1, there]))
        if images != texts:
            part = jnp.where(j < count_b, part, 0.0)
        if k == 0 and j == 0:
            row = lax.broadcasted_iota(jnp.int32, (pair, pair), 0)
            col = lax.broadcasted_iota(jnp.int32, (pair, pair), 1)
            part = part - (col == lax.rem(row + pair // 2, pair)).astype(F32)
        parts.append(part.astype(BF16))
    weights = jnp.concatenate(parts, axis=1)
    return scale[0] * jnp.dot(weights, b_all[...], preferred_element_type=F32)


def send_kernel(images, texts, logits, column, lse_b, b_all, scale, *outs):
    pair, width = column.shape[1], b_all.shape[1]
    rest = jnp.max(lse_b[1:2], axis=1, keepdims=True)
    row = lax.broadcasted_iota(jnp.int32, (TAIL, width), 0)
    tail = jnp.zeros((TAIL, width), F32)
    for i in range(3):
        piece = rest.astype(BF16).astype(F32)
        tail = jnp.where(row == i, piece, tail)
        rest = rest - piece
    tail = tail.astype(BF16)
    for k, out in enumerate(outs, 1):
        out[0:pair] = weigh(images, texts, k, logits, column, lse_b, b_all, scale).astype(BF16)
        out[pair:] = tail


def keep_kernel(images, texts, logits, column, lse_b, b_all, scale, out):
    out[...] = weigh(images, texts, 0, logits, column, lse_b, b_all, scale)


def reduce_kernel(images, texts, image, text, kept, lse_b, *refs):
    n = max(images, texts)
    got, message, grad_a = refs[: n - 1], *refs[n - 1 :]
    pair = kept.shape[0]
    own = pair // 2
    first = is_first()
    total = kept[...]
    excess = lse_b[1:2, 0:1]
    for ref in got:
        total = total + ref[0:pair].astype(F32)
        excess = excess + jnp.sum(ref[pair:].astype(F32), axis=0, keepdims=True)[:, 0:1]
    message[0:own] = total[own:]
    message[own:] = jnp.broadcast_to(excess, (8, message.shape[1]))
    unit, length = normalize(jnp.where(first, image[...].astype(F32), text[...].astype(F32)))
    grad_a[...] = unnormalize(unit, length, total[:own])


def finish_kernel(batch, image, text, message, grad_a, received, loss, grad_image, grad_text):
    own = image.shape[0]
    first = is_first()
    total = jnp.sum(message[own : own + 1, 0:1]) + jnp.sum(received[own : own + 1, 0:1])
    loss[0] = total / (2 * batch)
    unit, length = normalize(jnp.where(first, text[...].astype(F32), image[...].astype(F32)))
    grad_b = unnormalize(unit, length, received[:own])

    @pl.when(first)
    def _():
        grad_image[...] = grad_a[...]
        grad_text[...] = grad_b

    @pl.when(jnp.logical_not(first))
    def _():
        grad_image[...] = grad_b
        grad_text[...] = grad_a[...]


def on_device(image, text, logit_scale):
    devices = lax.axis_size("row") * lax.axis_size("col")
    images, texts = split(devices // 2)
    n = max(images, texts)
    core_pairs, group_pairs = permutes(devices)
    swap = lambda value: lax.ppermute(value, AXES, core_pairs)
    on_group = lambda value, k: lax.ppermute(value, AXES, group_pairs[k - 1])
    own, width = image.shape
    pair = 2 * own
    side = n * pair

    load = pl.CostEstimate(flops=0, transcendentals=0, bytes_accessed=4 * own * width)
    other_image, other_text = swap(image), swap(text)
    image, text, own_image, own_text = call(
        load_kernel,
        tuple(shape((own, width), BF16) for _ in range(4)),
        tuple(pltpu.with_memory_space_constraint(x, pltpu.HBM) for x in (image, text)),
        [pl.BlockSpec(memory_space=pltpu.HBM)] * 2,
        cost=load,
        scratch=[pltpu.SemaphoreType.DMA((2,))],
    )
    a_chip, b_chip = call(
        prepare_kernel,
        (shape((pair, width), BF16), shape((pair, width), BF16)),
        (own_image, own_text, other_image, other_text),
    )
    scale, a_chip = lax.optimization_barrier((logit_scale, a_chip))
    matmul = pl.CostEstimate(
        flops=2 * side * side * width, transcendentals=0, bytes_accessed=4 * side * side
    )
    a_blocks = [a_chip] + [on_group(a_chip, k) for k in range(1, n)]
    b_blocks = [b_chip] + [swap(a) for a in a_blocks[1:]]
    stats = call(
        functools.partial(stats_kernel, images, texts, n - 1),
        shape((8, side)),
        (*a_blocks, *b_blocks[:-1], scale),
        [VMEM] * (2 * n - 1) + [SMEM],
        cost=matmul,
    )
    stats = call(
        functools.partial(stats_kernel, images, texts, 1),
        shape((8, side)),
        (*a_blocks, b_blocks[-1], stats, scale),
        [VMEM] * (n + 2) + [SMEM],
    )
    got = [stats] + [on_group(stats, k) for k in range(1, n)]
    logits, b_all = call(
        functools.partial(logits_kernel, n),
        (shape((side, side)), shape((side, width), BF16)),
        (*a_blocks, *b_blocks, scale),
        [VMEM] * (2 * n) + [SMEM],
        cost=matmul,
    )
    lse_message, column = call(
        functools.partial(combine_kernel, images, texts),
        (shape((8, side)), shape((side, pair))),
        tuple(got),
    )
    lse_b = swap(lse_message)
    inputs = (logits, column, lse_b, b_all, scale)
    sends = call(
        functools.partial(send_kernel, images, texts),
        tuple(shape((pair + TAIL, width), BF16) for _ in range(1, n)),
        inputs,
        [VMEM] * 4 + [SMEM],
    )
    received = [on_group(sends[k - 1], k) for k in range(1, n)]
    kept = call(
        functools.partial(keep_kernel, images, texts), shape((pair, width)), inputs, [VMEM] * 4 + [SMEM], cost=matmul
    )
    message, grad_a = call(
        functools.partial(reduce_kernel, images, texts),
        (shape((own + 8, width)), shape((own, width))),
        (image, text, kept, lse_b, *received),
    )
    return call(
        functools.partial(finish_kernel, own * devices),
        (shape((1,)), shape((own, width)), shape((own, width))),
        (image, text, message, grad_a, swap(message)),
        out_specs=(SMEM, VMEM, VMEM),
    )


def solution(mesh):
    placed = (P(AXES, None), P(AXES, None), P())
    return jax.shard_map(
        on_device,
        mesh=mesh,
        in_specs=placed,
        out_specs=(P(), P(AXES, None), P(AXES, None)),
        check_vma=False,
    )
```

```python
import functools

import jax
import jax.numpy as jnp
from jax import lax
from jax.experimental import pallas as pl
from jax.experimental.pallas import tpu as pltpu
from jax.sharding import PartitionSpec as P

AXES = ("row", "col")
F32, BF16 = jnp.float32, jnp.bfloat16
VMEM = pl.BlockSpec(memory_space=pltpu.VMEM)
SMEM = pl.BlockSpec(memory_space=pltpu.SMEM)
TAIL = 8


def split(chips):
    bits = chips.bit_length() - 1
    images = 1 << (bits // 2)
    return images, chips // images


IMAGE_BASIS = (3, 1)
TEXT_BASIS = (3, 1)


def member(k, basis):
    mask = 0
    for bit in range(k.bit_length()):
        if k >> bit & 1:
            mask ^= basis[bit] if bit < len(basis) else 1 << bit
    return mask


def permutes(devices):
    images, texts = split(devices // 2)
    image_basis = IMAGE_BASIS if images >= 4 else ()
    text_basis = TEXT_BASIS if texts >= 4 else ()
    core = [(i, i ^ 1) for i in range(devices)]
    groups = []
    for k in range(1, max(images, texts)):
        pairs = []
        for i in range(devices):
            if i & 1 == 0 and k < images:
                pairs.append((i, i ^ (member(k, image_basis) << 1)))
            if i & 1 == 1 and k < texts:
                pairs.append((i, i ^ (member(k, text_basis) * images << 1)))
        groups.append(pairs)
    return core, groups


def normalize(embedding):
    values = embedding.astype(F32)
    length = jnp.sqrt(jnp.sum(values * values, axis=1, keepdims=True) + 1e-06)
    return (values / length, length)


def unnormalize(unit_rows, length, gradient):
    return (gradient - unit_rows * jnp.sum(unit_rows * gradient, axis=1, keepdims=True)) / length


def is_first():
    return lax.axis_index("col") % 2 == 0


def counts(images, texts):
    first = is_first()
    return jnp.where(first, images, texts), jnp.where(first, texts, images)


def call(kernel, outs, args, specs=None, out_specs=None, cost=None, scratch=(), limit=48 << 20):
    return pl.pallas_call(
        kernel,
        out_shape=outs,
        in_specs=specs or [VMEM] * len(args),
        out_specs=out_specs or jax.tree.map(lambda _: VMEM, outs),
        scratch_shapes=scratch,
        cost_estimate=cost,
        compiler_params=pltpu.CompilerParams(vmem_limit_bytes=limit),
    )(*args)


def shape(dims, dtype=F32):
    return jax.ShapeDtypeStruct(dims, dtype)


def load_kernel(image_hbm, text_hbm, image, text, own_image, own_text, arrived):
    copies = [
        pltpu.make_async_copy(source, target, arrived.at[i])
        for i, (source, target) in enumerate(((image_hbm, image), (text_hbm, text)))
    ]
    for copy in copies:
        copy.start()
    copies[0].wait()
    own_image[...] = normalize(image[...])[0].astype(BF16)
    copies[1].wait()
    own_text[...] = normalize(text[...])[0].astype(BF16)


def prepare_kernel(image, text, other_image, other_text, a_chip, b_chip):
    own = image.shape[0]
    img, txt = image[...], text[...]
    img_far, txt_far = normalize(other_image[...])[0].astype(BF16), normalize(other_text[...])[0].astype(BF16)
    first = is_first()

    @pl.when(first)
    def _():
        a_chip[0:own], a_chip[own:] = img, img_far
        b_chip[0:own], b_chip[own:] = txt_far, txt

    @pl.when(jnp.logical_not(first))
    def _():
        a_chip[0:own], a_chip[own:] = txt, txt_far
        b_chip[0:own], b_chip[own:] = img_far, img


def stats_kernel(images, texts, n_b, *refs):
    n = max(images, texts)
    last = n_b == 1 and n > 1
    a_in, b_in, rest = refs[:n], refs[n : n + n_b], refs[n + n_b :]
    before = rest[0] if last else None
    scale, stats = rest[-2:]
    pair = a_in[0].shape[0]
    s = scale[0]
    count_b = counts(images, texts)[1]
    for k in range(n):
        here = slice(k * pair, (k + 1) * pair)
        blocks = []
        for j in range(n_b):
            block = s * lax.dot_general(
                b_in[j][...], a_in[k][...], (((1,), (1,)), ((), ())), preferred_element_type=F32
            )
            if images != texts:
                block = jnp.where((n - 1 if last else j) < count_b, block, -1e30)
            blocks.append(block)
        peak = functools.reduce(jnp.maximum, blocks)
        peak = jnp.max(peak, axis=0, keepdims=True)
        if last:
            peak = jnp.maximum(peak, before[0:1, here])
        total = sum(jnp.exp(block - peak) for block in blocks)
        total = jnp.sum(total, axis=0, keepdims=True)
        if last:
            total = total + before[1:2, here] * jnp.exp(before[0:1, here] - peak)
        if last:
            stats[k : k + 1] = peak + jnp.log(total)
        else:
            stats[0:1, here] = peak
            stats[1:2, here] = total
        if k == 0 and last:
            stats[n : n + 1] = before[2:3, here]
        elif k == 0:
            row = lax.broadcasted_iota(jnp.int32, (pair, pair), 0)
            col = lax.broadcasted_iota(jnp.int32, (pair, pair), 1)
            paired = row == lax.rem(col + pair // 2, pair)
            stats[2:3, here] = jnp.sum(jnp.where(paired, blocks[0], 0.0), axis=0, keepdims=True)


def logits_kernel(n, *refs):
    a_in, b_in, (scale, logits, b_all) = refs[:n], refs[n : 2 * n], refs[2 * n :]
    pair = a_in[0].shape[0]
    for k in range(n):
        b_all[k * pair : (k + 1) * pair] = b_in[k][...]
    for k in range(n):
        logits[k * pair : (k + 1) * pair] = scale[0] * lax.dot_general(
            a_in[k][...], b_all[...], (((1,), (1,)), ((), ())), preferred_element_type=F32
        )


def combine_kernel(images, texts, *refs):
    n = max(images, texts)
    got, message, column = refs[:n], *refs[n:]
    pair = message.shape[1]
    count_a = counts(images, texts)[0]
    excess = jnp.zeros((1, pair), F32)
    for j in range(n):
        parts = []
        for k in range(n):
            part = got[k][(j ^ k) : (j ^ k) + 1]
            parts.append(jnp.where(k < count_a, part, -1e30) if images != texts else part)
        highest = functools.reduce(jnp.maximum, parts)
        lse = highest + jnp.log(sum(jnp.exp(part - highest) for part in parts))
        message[j : j + 1] = lse
        column[j * pair : (j + 1) * pair] = jnp.broadcast_to(lse, (pair, pair)).T
        over = lse - got[j][n : n + 1]
        excess = excess + (jnp.where(j < count_a, over, 0.0) if images != texts else over)
    message[n : n + 1] = jnp.broadcast_to(jnp.sum(excess, axis=1, keepdims=True), (1, pair))


def weigh(images, texts, k, logits, column, lse_b, b_all, scale):
    n = max(images, texts)
    pair = column.shape[1]
    here = slice(k * pair, (k + 1) * pair)
    count_b = counts(images, texts)[1]
    parts = []
    for j in range(n):
        there = slice(j * pair, (j + 1) * pair)
        block = logits[here, there]
        part = 0.5 * (jnp.exp(block - column[here]) + jnp.exp(block - lse_b[j : j + 1]))
        if images != texts:
            part = jnp.where(j < count_b, part, 0.0)
        if k == 0 and j == 0:
            row = lax.broadcasted_iota(jnp.int32, (pair, pair), 0)
            col = lax.broadcasted_iota(jnp.int32, (pair, pair), 1)
            part = part - (col == lax.rem(row + pair // 2, pair)).astype(F32)
        parts.append(part.astype(BF16))
    weights = jnp.concatenate(parts, axis=1)
    return scale[0] * jnp.dot(weights, b_all[...], preferred_element_type=F32)


def send_kernel(images, texts, logits, column, lse_b, b_all, scale, *outs):
    n = max(images, texts)
    pair, width = column.shape[1], b_all.shape[1]
    rest = lse_b[n : n + 1]
    row = lax.broadcasted_iota(jnp.int32, (TAIL, pair), 0)
    tail = jnp.zeros((TAIL, pair), F32)
    for i in range(3):
        piece = rest.astype(BF16).astype(F32)
        tail = jnp.where(row == i, piece, tail)
        rest = rest - piece
    for k, out in enumerate(outs, 1):
        block = weigh(images, texts, k, logits, column, lse_b, b_all, scale).astype(BF16)
        for c in range(width // pair):
            out[c * pair : (c + 1) * pair] = block[:, c * pair : (c + 1) * pair]
        out[width:] = tail.astype(BF16)


def keep_kernel(images, texts, logits, column, lse_b, b_all, scale, out):
    out[...] = weigh(images, texts, 0, logits, column, lse_b, b_all, scale)


def reduce_kernel(images, texts, image, text, kept, lse_b, *refs):
    n = max(images, texts)
    got, message, grad_a = refs[: n - 1], *refs[n - 1 :]
    pair, width = kept.shape
    own = pair // 2
    first = is_first()
    total = kept[...]
    excess = lse_b[n : n + 1, 0:1]
    for ref in got:
        chunks = [ref[c * pair : (c + 1) * pair] for c in range(width // pair)]
        total = total + jnp.concatenate(chunks, axis=1).astype(F32)
        excess = excess + jnp.sum(ref[width:].astype(F32), axis=0, keepdims=True)[:, 0:1]
    message[0:own] = total[own:]
    message[own:] = jnp.broadcast_to(excess, (8, message.shape[1]))
    unit, length = normalize(jnp.where(first, image[...].astype(F32), text[...].astype(F32)))
    grad_a[...] = unnormalize(unit, length, total[:own])


def finish_kernel(batch, image, text, message, grad_a, received, loss, grad_image, grad_text):
    own = image.shape[0]
    first = is_first()
    total = jnp.sum(message[own : own + 1, 0:1]) + jnp.sum(received[own : own + 1, 0:1])
    loss[0] = total / (2 * batch)
    unit, length = normalize(jnp.where(first, text[...].astype(F32), image[...].astype(F32)))
    grad_b = unnormalize(unit, length, received[:own])

    @pl.when(first)
    def _():
        grad_image[...] = grad_a[...]
        grad_text[...] = grad_b

    @pl.when(jnp.logical_not(first))
    def _():
        grad_image[...] = grad_b
        grad_text[...] = grad_a[...]


def on_device(image, text, logit_scale):
    devices = lax.axis_size("row") * lax.axis_size("col")
    images, texts = split(devices // 2)
    n = max(images, texts)
    core_pairs, group_pairs = permutes(devices)
    swap = lambda value: lax.ppermute(value, AXES, core_pairs)
    on_group = lambda value, k: lax.ppermute(value, AXES, group_pairs[k - 1])
    own, width = image.shape
    pair = 2 * own
    side = n * pair

    load = pl.CostEstimate(flops=0, transcendentals=0, bytes_accessed=4 * own * width)
    other_image, other_text = swap(image), swap(text)
    image, text, own_image, own_text = call(
        load_kernel,
        tuple(shape((own, width), BF16) for _ in range(4)),
        tuple(pltpu.with_memory_space_constraint(x, pltpu.HBM) for x in (image, text)),
        [pl.BlockSpec(memory_space=pltpu.HBM)] * 2,
        cost=load,
        scratch=[pltpu.SemaphoreType.DMA((2,))],
    )
    a_chip, b_chip = call(
        prepare_kernel,
        (shape((pair, width), BF16), shape((pair, width), BF16)),
        (own_image, own_text, other_image, other_text),
    )
    scale, a_chip = lax.optimization_barrier((logit_scale, a_chip))
    matmul = pl.CostEstimate(
        flops=2 * side * side * width, transcendentals=0, bytes_accessed=4 * side * side
    )
    a_blocks = [a_chip] + [on_group(a_chip, k) for k in range(1, n)]
    b_blocks = [b_chip] + [swap(a) for a in a_blocks[1:]]
    stats = call(
        functools.partial(stats_kernel, images, texts, n - 1),
        shape((8, side)),
        (*a_blocks, *b_blocks[:-1], scale),
        [VMEM] * (2 * n - 1) + [SMEM],
        cost=matmul,
    )
    rows = -(-(n + 1) // 8) * 8
    stats = call(
        functools.partial(stats_kernel, images, texts, 1),
        shape((rows, pair)),
        (*a_blocks, b_blocks[-1], stats, scale),
        [VMEM] * (n + 2) + [SMEM],
    )
    got = [stats] + [on_group(stats, k) for k in range(1, n)]
    logits, b_all = call(
        functools.partial(logits_kernel, n),
        (shape((side, side)), shape((side, width), BF16)),
        (*a_blocks, *b_blocks, scale),
        [VMEM] * (2 * n) + [SMEM],
        cost=matmul,
    )
    lse_message, column = call(
        functools.partial(combine_kernel, images, texts),
        (shape((rows, pair)), shape((side, pair))),
        tuple(got),
    )
    lse_b = swap(lse_message)
    inputs = (logits, column, lse_b, b_all, scale)
    sends = call(
        functools.partial(send_kernel, images, texts),
        tuple(shape((width + TAIL, pair), BF16) for _ in range(1, n)),
        inputs,
        [VMEM] * 4 + [SMEM],
    )
    received = [on_group(sends[k - 1], k) for k in range(1, n)]
    kept = call(
        functools.partial(keep_kernel, images, texts), shape((pair, width)), inputs, [VMEM] * 4 + [SMEM], cost=matmul
    )
    message, grad_a = call(
        functools.partial(reduce_kernel, images, texts),
        (shape((own + 8, width)), shape((own, width))),
        (image, text, kept, lse_b, *received),
    )
    return call(
        functools.partial(finish_kernel, own * devices),
        (shape((1,)), shape((own, width)), shape((own, width))),
        (image, text, message, grad_a, swap(message)),
        out_specs=(SMEM, VMEM, VMEM),
    )


def solution(mesh):
    placed = (P(AXES, None), P(AXES, None), P())
    return jax.shard_map(
        on_device,
        mesh=mesh,
        in_specs=placed,
        out_specs=(P(), P(AXES, None), P(AXES, None)),
        check_vma=False,
    )
```

```python
import functools

import jax
import jax.numpy as jnp
from jax import lax
from jax.experimental import pallas as pl
from jax.experimental.pallas import tpu as pltpu
from jax.sharding import PartitionSpec as P


AXES = ("row", "col")
F32, BF16 = jnp.float32, jnp.bfloat16
VMEM = pl.BlockSpec(memory_space=pltpu.VMEM)
SMEM = pl.BlockSpec(memory_space=pltpu.SMEM)
TAIL = 8


def split(chips):
    bits = chips.bit_length() - 1
    images = 1 << (bits // 2)
    return images, chips // images


IMAGE_BASIS = (3, 1)
TEXT_BASIS = (3, 1)


def member(k, basis):
    mask = 0
    for bit in range(k.bit_length()):
        if k >> bit & 1:
            mask ^= basis[bit] if bit < len(basis) else 1 << bit
    return mask


def permutes(devices):
    images, texts = split(devices // 2)
    image_basis = IMAGE_BASIS if images >= 4 else ()
    text_basis = TEXT_BASIS if texts >= 4 else ()
    core = [(i, i ^ 1) for i in range(devices)]
    groups = []
    for k in range(1, max(images, texts)):
        pairs = []
        for i in range(devices):
            if i & 1 == 0 and k < images:
                pairs.append((i, i ^ (member(k, image_basis) << 1)))
            if i & 1 == 1 and k < texts:
                pairs.append((i, i ^ (member(k, text_basis) * images << 1)))
        groups.append(pairs)
    return core, groups


def normalize(embedding):
    values = embedding.astype(F32)
    length = jnp.sqrt(jnp.sum(values * values, axis=1, keepdims=True) + 1e-06)
    return (values / length, length)


def unnormalize(unit_rows, length, gradient):
    return (gradient - unit_rows * jnp.sum(unit_rows * gradient, axis=1, keepdims=True)) / length


def is_first():
    return lax.axis_index("col") % 2 == 0


def counts(images, texts):
    first = is_first()
    return jnp.where(first, images, texts), jnp.where(first, texts, images)


def call(kernel, outs, args, specs=None, out_specs=None, cost=None, scratch=(), limit=48 << 20):
    return pl.pallas_call(
        kernel,
        out_shape=outs,
        in_specs=specs or [VMEM] * len(args),
        out_specs=out_specs or jax.tree.map(lambda _: VMEM, outs),
        scratch_shapes=scratch,
        cost_estimate=cost,
        compiler_params=pltpu.CompilerParams(vmem_limit_bytes=limit),
    )(*args)


def shape(dims, dtype=F32):
    return jax.ShapeDtypeStruct(dims, dtype)


def load_kernel(image_hbm, text_hbm, image, text, own_image, own_text, arrived):
    copies = [
        pltpu.make_async_copy(source, target, arrived.at[i])
        for i, (source, target) in enumerate(((image_hbm, image), (text_hbm, text)))
    ]
    for copy in copies:
        copy.start()
    copies[0].wait()
    own_image[...] = normalize(image[...])[0].astype(BF16)
    copies[1].wait()
    own_text[...] = normalize(text[...])[0].astype(BF16)


def prepare_kernel(image, text, other_image, other_text, a_chip, b_chip):
    own = image.shape[0]
    img, txt = image[...], text[...]
    img_far, txt_far = normalize(other_image[...])[0].astype(BF16), normalize(other_text[...])[0].astype(BF16)
    first = is_first()

    @pl.when(first)
    def _():
        a_chip[0:own], a_chip[own:] = img, img_far
        b_chip[0:own], b_chip[own:] = txt_far, txt

    @pl.when(jnp.logical_not(first))
    def _():
        a_chip[0:own], a_chip[own:] = txt, txt_far
        b_chip[0:own], b_chip[own:] = img_far, img


def scale_kernel(scale, row):
    row[...] = jnp.full(row.shape, scale[0], F32)


def units_kernel(image, text, units, lengths):
    own = image.shape[0]
    first = is_first()
    img, txt = image[...].astype(F32), text[...].astype(F32)
    for i, raw in enumerate((jnp.where(first, img, txt), jnp.where(first, txt, img))):
        unit, length = normalize(raw)
        units[i * own : (i + 1) * own] = unit
        lengths[i * own : (i + 1) * own] = jnp.broadcast_to(length, (own, lengths.shape[1]))


def stats_kernel(images, texts, n_b, *refs):
    n = max(images, texts)
    last = n_b == 1 and n > 1
    a_in, b_in, rest = refs[:n], refs[n : n + n_b], refs[n + n_b :]
    before = rest[0] if last else None
    scale, stats = rest[-2:]
    pair = a_in[0].shape[0]
    s = scale[0:1]
    count_b = counts(images, texts)[1]
    for k in range(n):
        here = slice(k * pair, (k + 1) * pair)
        blocks = []
        for j in range(n_b):
            block = s * lax.dot_general(
                b_in[j][...], a_in[k][...], (((1,), (1,)), ((), ())), preferred_element_type=F32
            )
            if images != texts:
                block = jnp.where((n - 1 if last else j) < count_b, block, -1e30)
            blocks.append(block)
        peak = functools.reduce(jnp.maximum, blocks)
        peak = jnp.max(peak, axis=0, keepdims=True)
        if last:
            peak = jnp.maximum(peak, before[0:1, here])
        total = sum(jnp.exp(block - peak) for block in blocks)
        total = jnp.sum(total, axis=0, keepdims=True)
        if last:
            total = total + before[1:2, here] * jnp.exp(before[0:1, here] - peak)
        if last:
            stats[k : k + 1] = peak + jnp.log(total)
        else:
            stats[0:1, here] = peak
            stats[1:2, here] = total
        if k == 0 and last:
            stats[n : n + 1] = before[2:3, here]
        elif k == 0:
            row = lax.broadcasted_iota(jnp.int32, (pair, pair), 0)
            col = lax.broadcasted_iota(jnp.int32, (pair, pair), 1)
            paired = row == lax.rem(col + pair // 2, pair)
            stats[2:3, here] = jnp.sum(jnp.where(paired, blocks[0], 0.0), axis=0, keepdims=True)


def logits_kernel(n, *refs):
    a_in, b_in, (scale, logits, b_all) = refs[:n], refs[n : 2 * n], refs[2 * n :]
    pair = a_in[0].shape[0]
    for k in range(n):
        b_all[k * pair : (k + 1) * pair] = b_in[k][...]
    for k in range(n):
        logits[k * pair : (k + 1) * pair] = scale[0:1, 0:1] * lax.dot_general(
            a_in[k][...], b_all[...], (((1,), (1,)), ((), ())), preferred_element_type=F32
        )


def combine_kernel(images, texts, *refs):
    n = max(images, texts)
    got, message, column = refs[:n], *refs[n:]
    pair = message.shape[1]
    count_a = counts(images, texts)[0]
    excess = jnp.zeros((1, pair), F32)
    for j in range(n):
        parts = []
        for k in range(n):
            part = got[k][(j ^ k) : (j ^ k) + 1]
            parts.append(jnp.where(k < count_a, part, -1e30) if images != texts else part)
        highest = functools.reduce(jnp.maximum, parts)
        lse = highest + jnp.log(sum(jnp.exp(part - highest) for part in parts))
        message[j : j + 1] = lse
        column[j * pair : (j + 1) * pair] = jnp.broadcast_to(lse, (pair, pair)).T
        over = lse - got[j][n : n + 1]
        excess = excess + (jnp.where(j < count_a, over, 0.0) if images != texts else over)
    message[n : n + 1] = jnp.broadcast_to(jnp.sum(excess, axis=1, keepdims=True), (1, pair))


def weigh(images, texts, k, logits, column, lse_b, b_all, scale):
    n = max(images, texts)
    pair = column.shape[1]
    here = slice(k * pair, (k + 1) * pair)
    count_b = counts(images, texts)[1]
    parts = []
    for j in range(n):
        there = slice(j * pair, (j + 1) * pair)
        block = logits[here, there]
        part = 0.5 * (jnp.exp(block - column[here]) + jnp.exp(block - lse_b[j : j + 1]))
        if images != texts:
            part = jnp.where(j < count_b, part, 0.0)
        if k == 0 and j == 0:
            row = lax.broadcasted_iota(jnp.int32, (pair, pair), 0)
            col = lax.broadcasted_iota(jnp.int32, (pair, pair), 1)
            part = part - (col == lax.rem(row + pair // 2, pair)).astype(F32)
        parts.append(part.astype(BF16))
    weights = jnp.concatenate(parts, axis=1)
    return scale[0:1, 0:1] * jnp.dot(weights, b_all[...], preferred_element_type=F32)


def send_kernel(images, texts, logits, column, lse_b, b_all, scale, *outs):
    n = max(images, texts)
    pair, width = column.shape[1], b_all.shape[1]
    rest = lse_b[n : n + 1]
    row = lax.broadcasted_iota(jnp.int32, (TAIL, pair), 0)
    tail = jnp.zeros((TAIL, pair), F32)
    for i in range(3):
        piece = rest.astype(BF16).astype(F32)
        tail = jnp.where(row == i, piece, tail)
        rest = rest - piece
    for k, out in enumerate(outs, 1):
        block = weigh(images, texts, k, logits, column, lse_b, b_all, scale).astype(BF16)
        for c in range(width // pair):
            out[c * pair : (c + 1) * pair] = block[:, c * pair : (c + 1) * pair]
        out[width:] = tail.astype(BF16)


def keep_kernel(images, texts, logits, column, lse_b, b_all, scale, out):
    out[...] = weigh(images, texts, 0, logits, column, lse_b, b_all, scale)


def reduce_kernel(images, texts, units, lengths, kept, lse_b, *refs):
    n = max(images, texts)
    got, message, grad_a = refs[: n - 1], *refs[n - 1 :]
    pair, width = kept.shape
    own = pair // 2
    total = kept[...]
    excess = lse_b[n : n + 1, 0:1]
    for ref in got:
        chunks = [ref[c * pair : (c + 1) * pair] for c in range(width // pair)]
        total = total + jnp.concatenate(chunks, axis=1).astype(F32)
        excess = excess + jnp.sum(ref[width:].astype(F32), axis=0, keepdims=True)[:, 0:1]
    message[0:own] = total[own:]
    message[own:] = jnp.broadcast_to(excess, (8, message.shape[1]))
    grad_a[...] = unnormalize(units[:own], lengths[:own, 0:1], total[:own])


def finish_kernel(batch, units, lengths, message, grad_a, received, loss, grad_image, grad_text):
    own = grad_a.shape[0]
    first = is_first()
    total = jnp.sum(message[own : own + 1, 0:1]) + jnp.sum(received[own : own + 1, 0:1])
    loss[0] = total / (2 * batch)
    grad_b = unnormalize(units[own:], lengths[own:, 0:1], received[:own])

    @pl.when(first)
    def _():
        grad_image[...] = grad_a[...]
        grad_text[...] = grad_b

    @pl.when(jnp.logical_not(first))
    def _():
        grad_image[...] = grad_b
        grad_text[...] = grad_a[...]


def on_device(image, text, logit_scale):
    devices = lax.axis_size("row") * lax.axis_size("col")
    images, texts = split(devices // 2)
    n = max(images, texts)
    core_pairs, group_pairs = permutes(devices)
    swap = lambda value: lax.ppermute(value, AXES, core_pairs)

    def on_group(value, k):
        return lax.ppermute(value, AXES, group_pairs[k - 1])

    own, width = image.shape
    pair = 2 * own
    side = n * pair

    load = pl.CostEstimate(flops=0, transcendentals=0, bytes_accessed=4 * own * width)
    other_image, other_text = swap(image), swap(text)
    image, text, own_image, own_text = call(
        load_kernel,
        tuple(shape((own, width), BF16) for _ in range(4)),
        tuple(pltpu.with_memory_space_constraint(x, pltpu.HBM) for x in (image, text)),
        [pl.BlockSpec(memory_space=pltpu.HBM)] * 2,
        cost=load,
        scratch=[pltpu.SemaphoreType.DMA((2,))],
    )
    a_chip, b_chip = call(
        prepare_kernel,
        (shape((pair, width), BF16), shape((pair, width), BF16)),
        (own_image, own_text, other_image, other_text),
    )
    scale = call(scale_kernel, shape((8, pair)), (logit_scale,), [SMEM])
    units, lengths = call(
        units_kernel, (shape((pair, width)), shape((pair, pair))), (image, text), cost=load
    )
    matmul = pl.CostEstimate(
        flops=2 * side * side * width, transcendentals=0, bytes_accessed=4 * side * side
    )
    a_blocks = [a_chip] + [on_group(a_chip, k) for k in range(1, n)]
    b_blocks = [b_chip] + [swap(a) for a in a_blocks[1:]]
    stats = call(
        functools.partial(stats_kernel, images, texts, n - 1),
        shape((8, side)),
        (*a_blocks, *b_blocks[:-1], scale),
        cost=matmul,
    )
    rows = -(-(n + 1) // 8) * 8
    stats = call(
        functools.partial(stats_kernel, images, texts, 1),
        shape((rows, pair)),
        (*a_blocks, b_blocks[-1], stats, scale),
    )
    got = [stats] + [on_group(stats, k) for k in range(1, n)]
    logits, b_all = call(
        functools.partial(logits_kernel, n),
        (shape((side, side)), shape((side, width), BF16)),
        (*a_blocks, *b_blocks, scale),
        cost=matmul,
    )
    lse_message, column = call(
        functools.partial(combine_kernel, images, texts),
        (shape((rows, pair)), shape((side, pair))),
        tuple(got),
    )
    lse_b = swap(lse_message)
    inputs = (logits, column, lse_b, b_all, scale)
    sends = call(
        functools.partial(send_kernel, images, texts),
        tuple(shape((width + TAIL, pair), BF16) for _ in range(1, n)),
        inputs,
    )
    received = [on_group(sends[k - 1], k) for k in range(1, n)]
    kept = call(
        functools.partial(keep_kernel, images, texts), shape((pair, width)), inputs, cost=matmul
    )
    message, grad_a = call(
        functools.partial(reduce_kernel, images, texts),
        (shape((own + 8, width)), shape((own, width))),
        (units, lengths, kept, lse_b, *received),
    )
    return call(
        functools.partial(finish_kernel, own * devices),
        (shape((1,)), shape((own, width)), shape((own, width))),
        (units, lengths, message, grad_a, swap(message)),
        out_specs=(SMEM, VMEM, VMEM),
    )


def solution(mesh):
    placed = (P(AXES, None), P(AXES, None), P())
    return jax.shard_map(
        on_device,
        mesh=mesh,
        in_specs=placed,
        out_specs=(P(), P(AXES, None), P(AXES, None)),
        check_vma=False,
    )
```
